256 devices in a mesh: tm: 8 (over x_lo, y), sta: 32 (over x_hi, z, core).
Axes of the slice: x: 4 (x_hi: 2, x_lo: 2; x = x_hi * 2 + x_lo), y: 4, z: 8, core: 2. Of those that a mesh axis runs over, the one named last changes fastest.
Arguments:
- templates: bfloat16 [8, 256, 32, 3, 600], P('tm', None, 'sta'), may hold values from -6 to 6
- channel_mask: int32 [8, 256, 32], P('tm', None, 'sta'), may hold values 0 or 1
- waveforms: bfloat16 [32, 3, 7168], P('sta', None, 'tm'), may hold values from -60 to 60
- waveform_tail: bfloat16 [32, 3, 599], P('sta'), may hold values from -6 to 6
Outputs:
- detections: float32 [8, 256, 7168], P(None, 'sta', 'tm')
The draws below stay inside these ranges and needn't reach their ends.
All inputs are finite; a program needn't handle non-finite values. No bound on the sum of `channel_mask` on one device may be relied on, other than what follows from the above.
Results may differ from the reference program's by a relative error of at most 0.0044.
Values may be sent and summed in bfloat16 or wider, within the bound.
A program may use at most 128 MiB of HBM per device.

```python
import math
import jax
import jax.numpy as jnp
from jax import lax

L = 600
TPL_DEV = 256
TBLOCKS = 8
TEMPLATES = 2048
STATIONS = 32
SAMPLES = 7168
HALO = 599


def draw_waveforms(key, part):
    noise_key = jax.random.fold_in(key, 11)
    level_key = jax.random.fold_in(key, 12)
    array_shape = (STATIONS, 3, SAMPLES)
    noise = jax.random.truncated_normal(noise_key, -6.0, 6.0, array_shape, jnp.float32)
    levels = jax.random.uniform(level_key, (STATIONS, 3, SAMPLES // 64, 1), jnp.float32, 0.0, math.log(10.0))
    envelope = jnp.broadcast_to(jnp.exp(levels), (STATIONS, 3, SAMPLES // 64, 64)).reshape(array_shape)
    return (noise * envelope).astype(jnp.bfloat16)


def set_ends(result, own_key, smallest, top_value):
    extent = result.shape
    spot = [jax.random.randint(jax.random.fold_in(own_key, axis), (), 0, extent[axis]) for axis in range(len(extent))]
    result = result.at[tuple(spot)].set(smallest)
    longest = extent.index(max(extent))
    spot[longest] = (spot[longest] + 1) % extent[longest]
    return result.at[tuple(spot)].set(top_value)


def with_spikes(result, stream_key, source, target, parts, factor):
    def block_of(axis_at):
        return (jnp.arange(result.shape[axis_at]) // (result.shape[axis_at] // parts)).reshape((-1,) + (1,) * (result.ndim - 1 - axis_at))

    first = jax.random.permutation(stream_key, parts)[block_of(target)]
    second = (block_of(target) + parts // 2) % parts
    return jnp.where((block_of(source) == first) | (block_of(source) == second), factor * result, result)


def shard_levels(own_key, dims, cuts, least, largest):
    gain = 1.0
    for dim, blocks in cuts:
        steps = jax.random.uniform(jax.random.fold_in(jax.random.fold_in(own_key, 6), dim), (blocks,), jnp.float32, least / len(cuts), largest / len(cuts))
        gain = gain * jnp.repeat(jnp.exp(steps), dims[dim] // blocks).reshape((-1,) + (1,) * (len(dims) - 1 - dim))
    return gain


def scatter_about(rng, shape, scale, most, cuts=(), dtype=jnp.bfloat16):
    factor_of = shard_levels(rng, shape, cuts, -0.22, 0.18) if cuts else 1.0
    values = jax.random.normal(rng, shape, jnp.float32) * scale * factor_of
    return jnp.minimum(jnp.maximum(values, -most), most).astype(dtype)


def bell_draw_with(stream_key, extent, deviation, most, split, heavy, held_as=jnp.bfloat16):
    entries = deviation * jax.random.normal(stream_key, extent, jnp.float32)
    if split:
        entries = entries * shard_levels(stream_key, extent, split, -0.22, 0.18)
    return jnp.clip(with_spikes(entries, jax.random.fold_in(stream_key, 3), *heavy), -most, most).astype(held_as)


def setup_inputs(seed: int = 0) -> dict:
    arg_keys = jax.random.split(jax.random.key(seed), 5)
    return {
        "templates": bell_draw_with(arg_keys[0], (TBLOCKS, TPL_DEV, STATIONS, 3, L), 1.0, 6.0, ((0, 8), (2, 32)), (2, 1, 32, 2.75)),
        "channel_mask": set_ends((jax.random.randint(arg_keys[1], (TBLOCKS, TPL_DEV, STATIONS), 0, 4) < 3).astype(jnp.int32), jax.random.fold_in(arg_keys[1], 1), 0, 1),
        "waveforms": draw_waveforms(jax.random.fold_in(arg_keys[4], 71), 0),
        "waveform_tail": scatter_about(arg_keys[3], (STATIONS, 3, HALO), 1.0, 6.0, ((0, 32),)),
    }


def normalize(templates, channel_mask):
    values = templates.astype(jnp.float32)
    centred = values - lax.optimization_barrier(jnp.mean(values, axis=-1, keepdims=True))
    energy = lax.optimization_barrier(jnp.sum(centred * centred, axis=-1, keepdims=True))
    weighted = centred * lax.rsqrt(energy + 1e-05) * channel_mask.astype(jnp.float32)[..., None, None]
    return weighted.astype(jnp.bfloat16)

def windows(extended, length, sample_count):
    values = extended.astype(jnp.float32)
    zero_col = jnp.zeros(values.shape[:-1] + (1,), jnp.float32)
    prefix_one = jnp.concatenate([zero_col, jnp.cumsum(values, axis=-1)], axis=-1)
    prefix_two = jnp.concatenate([zero_col, jnp.cumsum(values * values, axis=-1)], axis=-1)
    window_sum = prefix_one[..., length:length + sample_count] - prefix_one[..., :sample_count]
    window_square = prefix_two[..., length:length + sample_count] - prefix_two[..., :sample_count]
    inverse = lax.rsqrt(window_square - window_sum * window_sum / length + 1e-05)
    span = extended.shape[-1]
    leading = extended.shape[:-1]
    copies = jnp.broadcast_to(extended[..., None, :], leading + (length + 1, span))
    flat = copies.reshape(leading + ((length + 1) * span,))
    hankel = flat[..., :length * (span + 1)].reshape(leading + (length, span + 1))[..., :sample_count]
    return (hankel.astype(jnp.float32) * inverse[..., None, :]).astype(jnp.bfloat16)

def reference(templates, channel_mask, waveforms, waveform_tail):
    normed = normalize(templates, channel_mask)
    tpl_flat = normed.reshape(TEMPLATES, STATIONS, 3 * L)
    moved = jnp.moveaxis(tpl_flat, 1, 0)
    extended = jnp.concatenate([waveforms, waveform_tail], axis=-1)

    def station(total, pieces):
        station_tpl, station_wave = pieces
        scaled = windows(station_wave, L, SAMPLES).reshape(3 * L, SAMPLES)
        return (total + jnp.dot(station_tpl, scaled, preferred_element_type=jnp.float32), None)
    start_total = jnp.zeros((TEMPLATES, SAMPLES), jnp.float32)
    total, unused = lax.scan(station, start_total, (moved, extended))
    return total.reshape(TBLOCKS, TPL_DEV, SAMPLES)
```

```python
import jax
import jax.numpy as jnp
from jax import lax
from jax.experimental import pallas as pl
from jax.experimental.pallas import tpu as pltpu
from jax.sharding import PartitionSpec as P

MESH = pl.DeviceIdType.MESH
LAGS = 600
KPAD = 640
CHUNK = 896
UNITS = 8
PAIRS = 4
WIDE = 8320
ROWS = 8192


def kernel(
    tpl_ref, mask_ref, wav_ref, tail_ref, out_ref,
    wrecv, xs, hankel, invb, tf, lhs, own, exs, exr, us, ur, ds_, dr, fown, xsend, xrecv, osend,
    w_ss, w_rs, e_ss, e_rs, u_ss, u_rs, d_ss, d_rs, x_ss, x_rs, o_ss, o_rs,
):
    t = lax.axis_index("tm")
    s = lax.axis_index("sta")
    h = s // 16
    z = (s // 2) % 8
    c = s % 2
    sib = h * 16 + z * 2 + (1 - c)
    up = h * 16 + ((z + 1) % 8) * 2 + c
    down = h * 16 + ((z + 7) % 8) * 2 + c
    across = (1 - h) * 16 + z * 2 + c

    barrier = pltpu.get_barrier_semaphore()
    for step in range(1, UNITS):
        pl.semaphore_signal(barrier, inc=1, device_id=((t + step) % UNITS, s), device_id_type=MESH)
    for other in (sib, up, down, across):
        pl.semaphore_signal(barrier, inc=1, device_id=(t, other), device_id_type=MESH)
    pl.semaphore_wait(barrier, 11)

    def remote(src, dst, ssem, rsem, dev):
        return pltpu.make_async_remote_copy(
            src_ref=src, dst_ref=dst, send_sem=ssem, recv_sem=rsem, device_id=dev, device_id_type=MESH
        )

    wcopies = [
        remote(wav_ref, wrecv.at[k], w_ss.at[k], w_rs.at[k], ((t + k) % UNITS, s)) for k in range(1, UNITS)
    ]
    for cp in wcopies:
        cp.start()

    maskf = mask_ref[...].astype(jnp.float32)
    for comp in range(3):
        values = tpl_ref[comp].astype(jnp.float32)
        mean = jnp.sum(values, axis=0, keepdims=True) / LAGS
        centred = values - mean
        energy = jnp.sum(centred * centred, axis=0, keepdims=True)
        normed = centred * lax.rsqrt(energy + 1e-05) * maskf
        padded = jnp.concatenate([normed, jnp.zeros((KPAD - LAGS, 256), jnp.float32)], axis=0)
        tf[...] = padded.T
        for o in range(2):
            for d in range(8):
                zz = (z + d) % 8
                cc = c if o == 0 else 1 - c
                first = pl.multiple_of((h * 16 + zz * 2 + cc) * 8, 8)
                second = pl.multiple_of(((1 - h) * 16 + zz * 2 + cc) * 8, 8)
                both = jnp.concatenate([tf[pl.ds(first, 8), :], tf[pl.ds(second, 8), :]], axis=0)
                lhs[comp, 16 * (8 * o + d) : 16 * (8 * o + d) + 16, :] = both.astype(jnp.bfloat16)

    xs[...] = jnp.zeros((8, WIDE), jnp.float32)

    def place(value, start, width):
        v = value.astype(jnp.float32)
        xs[0:3, pl.ds(start, width)] = v
        xs[4:7, pl.ds(start, width)] = v * v

    place(wav_ref[...], pl.multiple_of(t * CHUNK, 128), CHUNK)
    place(tail_ref[...], 8 * CHUNK, LAGS - 1)
    for k in range(1, UNITS):
        wcopies[k - 1].wait_recv()
        place(wrecv[k], pl.multiple_of(((t + UNITS - k) % UNITS) * CHUNK, 128), CHUNK)

    def window(k, carry):
        at = pl.multiple_of(k * 1024, 128)
        a = xs[:, pl.ds(at, 1664)]

        def ahead(v, n):
            return pltpu.roll(v, 1664 - n, axis=1)

        sums = {1: a}
        n = 1
        while n < 512:
            sums[2 * n] = sums[n] + ahead(sums[n], n)
            n *= 2
        total = sums[512] + ahead(sums[64], 512) + ahead(sums[16], 576) + ahead(sums[8], 592)
        total = total[:, :1024]
        squares = pltpu.roll(total, 4, axis=0)
        inverse = lax.rsqrt(squares - total * total / LAGS + 1e-05)
        for comp in range(3):
            invb[comp, :, pl.ds(at, 1024)] = jnp.broadcast_to(inverse[comp : comp + 1], (8, 1024))
        return carry

    lax.fori_loop(0, 7, window, 0)

    sub = lax.broadcasted_iota(jnp.int32, (8, 640), 0)

    def skewed(k, carry):
        at = pl.multiple_of(k * 512, 128)
        for comp in range(3):
            v = jnp.broadcast_to(xs[comp : comp + 1, pl.ds(at, 640)], (8, 640))
            for bit in (1, 2, 4):
                v = jnp.where((sub & bit) != 0, pltpu.roll(v, 640 - bit, axis=1), v)
            for m in range(8):
                lo = v if m == 0 else pltpu.roll(v, 640 - 16 * m, axis=1)
                hi = pltpu.roll(v, 640 - 16 * m - 8, axis=1)
                both = jnp.concatenate([lo[:, :512], hi[:, :512]], axis=0).astype(jnp.bfloat16)
                for q in range(4):
                    hankel[comp, pl.ds(pl.multiple_of(at + 128 * q + 16 * m, 16), 16), :] = both[
                        :, 128 * q : 128 * q + 128
                    ]
        return carry

    lax.fori_loop(0, 16, skewed, 0)

    def compute(pair):
        def tile(i, carry):
            where = []
            for j in range(2):
                b = 2 * i + j
                second = (b >= 7).astype(jnp.int32)
                unit = 2 * pair + second
                inside = b - 7 * second
                q = (t + unit + 1) % UNITS
                where.append((unit, inside, pl.multiple_of(q * CHUNK + inside * 128, 128)))
            acc = None
            for comp in range(3):
                rhs = jnp.concatenate([hankel[comp, pl.ds(w[2], KPAD), :] for w in where], axis=1)
                prod = jnp.dot(lhs[comp], rhs, preferred_element_type=jnp.float32)
                inv = jnp.concatenate([invb[comp, :, pl.ds(w[2], 128)] for w in where], axis=1)
                prod = prod.reshape(32, 8, 256) * inv[None]
                acc = prod if acc is None else acc + prod
            acc = acc.reshape(256, 256)
            for j in range(2):
                unit, inside, _ = where[j]
                lanes = pl.ds(pl.multiple_of(inside * 128, 128), 128)
                own[unit, :, lanes] = acc[:128, 128 * j : 128 * j + 128]
                exs[unit, :, lanes] = acc[128:, 128 * j : 128 * j + 128].astype(jnp.bfloat16)
            return carry

        lax.fori_loop(0, 7, tile, 0)

    ecopies = [
        remote(exs.at[pl.ds(2 * p, 2)], exr.at[pl.ds(2 * p, 2)], e_ss.at[p], e_rs.at[p], (t, sib)) for p in range(PAIRS)
    ]
    ucopies = [
        [remote(us.at[u, k], ur.at[u, k], u_ss.at[u, k], u_rs.at[u, k], (t, up)) for k in range(4)] for u in range(UNITS)
    ]
    dcopies = [
        [remote(ds_.at[u, k], dr.at[u, k], d_ss.at[u, k], d_rs.at[u, k], (t, down)) for k in range(4)]
        for u in range(UNITS)
    ]
    xcopies = [remote(xsend.at[p], xrecv.at[p], x_ss.at[p], x_rs.at[p], (t, across)) for p in range(PAIRS)]
    ocopies = [
        remote(osend.at[u], out_ref.at[t], o_ss.at[u], o_rs.at[u], ((t + u + 1) % UNITS, s)) for u in range(UNITS - 1)
    ]
    started = []

    def begin(cp):
        cp.start()
        started.append(cp)

    def chunk(u, d):
        return own[u, 16 * d : 16 * d + 16, :] + exr[u, 16 * d : 16 * d + 16, :].astype(jnp.float32)

    def stage(pair, k):
        units = (2 * pair, 2 * pair + 1)
        if k == 1:
            ecopies[pair].wait_recv()
            us[units[0], 0] = chunk(units[0], 4).astype(jnp.bfloat16)
            begin(ucopies[units[0]][0])
            ds_[units[1], 0] = chunk(units[1], 4).astype(jnp.bfloat16)
            begin(dcopies[units[1]][0])
        elif k <= 4:
            for u in units:
                for copies, send, recv, d, first in (
                    (ucopies, us, ur, 5 - k, u % 2 == 0),
                    (dcopies, ds_, dr, 3 + k, u % 2 == 1),
                ):
                    v = chunk(u, d)
                    if k > 2 or first:
                        copies[u][k - 2].wait_recv()
                        v = v + recv[u, k - 2].astype(jnp.float32)
                    send[u, k - 1] = v.astype(jnp.bfloat16)
                    begin(copies[u][k - 1])
        elif k == 5:
            away = []
            for u in units:
                ucopies[u][3].wait_recv()
                dcopies[u][3].wait_recv()
                v = chunk(u, 0) + ur[u, 3].astype(jnp.float32) + dr[u, 3].astype(jnp.float32)
                fown[u] = v[:8]
                away.append(v[8:])
            xsend[pair] = jnp.concatenate(away, axis=0).astype(jnp.bfloat16)
            begin(xcopies[pair])
        else:
            xcopies[pair].wait_recv()
            got = xrecv[pair].astype(jnp.float32)
            for j, u in enumerate(units):
                v = fown[u] + got[8 * j : 8 * j + 8]
                if u < UNITS - 1:
                    osend[u] = v
                    begin(ocopies[u])
                else:
                    out_ref[t] = v

    for slot in range(PAIRS + 6):
        if slot < PAIRS:
            compute(slot)
            begin(ecopies[slot])
        for k in range(6, 0, -1):
            pair = slot - k
            if 0 <= pair < PAIRS:
                stage(pair, k)

    for u in range(UNITS - 1):
        remote(
            osend.at[u], out_ref.at[(t + UNITS - u - 1) % UNITS], o_ss.at[u], o_rs.at[u], ((t + u + 1) % UNITS, s)
        ).wait_recv()
    for cp in wcopies + started:
        cp.wait_send()


def per_device(templates, channel_mask, waveforms, waveform_tail):
    tpl = jnp.transpose(templates[0, :, 0], (1, 2, 0))
    mask = channel_mask.reshape(1, 256)
    bf, f32 = jnp.bfloat16, jnp.float32
    dma = pltpu.SemaphoreType.DMA
    vmem = pl.BlockSpec(memory_space=pltpu.VMEM)
    return pl.pallas_call(
        kernel,
        out_shape=jax.ShapeDtypeStruct((UNITS, 8, CHUNK), f32),
        in_specs=[vmem] * 4,
        out_specs=vmem,
        scratch_shapes=[
            pltpu.VMEM((UNITS, 3, CHUNK), bf),
            pltpu.VMEM((8, WIDE), f32),
            pltpu.VMEM((3, ROWS, 128), bf),
            pltpu.VMEM((3, 8, UNITS * CHUNK), f32),
            pltpu.VMEM((256, KPAD), f32),
            pltpu.VMEM((3, 256, KPAD), bf),
            pltpu.VMEM((UNITS, 128, CHUNK), f32),
            pltpu.VMEM((UNITS, 128, CHUNK), bf),
            pltpu.VMEM((UNITS, 128, CHUNK), bf),
            pltpu.VMEM((UNITS, 4, 16, CHUNK), bf),
            pltpu.VMEM((UNITS, 4, 16, CHUNK), bf),
            pltpu.VMEM((UNITS, 4, 16, CHUNK), bf),
            pltpu.VMEM((UNITS, 4, 16, CHUNK), bf),
            pltpu.VMEM((UNITS, 8, CHUNK), f32),
            pltpu.VMEM((PAIRS, 16, CHUNK), bf),
            pltpu.VMEM((PAIRS, 16, CHUNK), bf),
            pltpu.VMEM((UNITS, 8, CHUNK), f32),
            dma((UNITS,)), dma((UNITS,)),
            dma((PAIRS,)), dma((PAIRS,)),
            dma((UNITS, 4)), dma((UNITS, 4)),
            dma((UNITS, 4)), dma((UNITS, 4)),
            dma((PAIRS,)), dma((PAIRS,)),
            dma((UNITS,)), dma((UNITS,)),
        ],
        compiler_params=pltpu.CompilerParams(
            collective_id=0, has_side_effects=True, vmem_limit_bytes=50 * 1024 * 1024
        ),
    )(tpl, mask, waveforms[0], waveform_tail[0])


def solution(mesh):
    placed = (
        P("tm", None, "sta", None, None),
        P("tm", None, "sta"),
        P("sta", None, "tm"),
        P("sta", None, None),
    )
    return jax.shard_map(
        per_device, mesh=mesh, in_specs=placed, out_specs=P(None, "sta", "tm"), check_vma=False
    )
```

```python
import jax
import jax.numpy as jnp
from jax import lax
from jax.experimental import pallas as pl
from jax.experimental.pallas import tpu as pltpu
from jax.sharding import PartitionSpec as P

MESH = pl.DeviceIdType.MESH
LAGS = 600
KPAD = 640
CHUNK = 896
UNITS = 8
TILES = 28
WIDE = 7936
BLOCKS = 60
TILE_US, EXCHANGE_US, HOP_US, QUEUE_US = 0.35, 1.0, 3.2, 0.2


def order_of_work():
    events = [(TILE_US * i, 0, ("tile", i)) for i in range(TILES)]
    for u in range(UNITS):
        done = TILE_US * (7 * (u // 2) + (4 if u % 2 == 0 else 7))
        for k in range(1, 6):
            when = done + EXCHANGE_US + HOP_US * (k - 1) + QUEUE_US * u * (k > 1)
            events.append((when, 1, ("stage", u, k)))
    return [e[2] for e in sorted(events, key=lambda e: (e[0], e[1], -e[2][-1]))]


def kernel(
    tpl_hbm, mask_hbm, wav_hbm, tail_hbm, out_ref,
    tpl_ref, mask_ref, wav_ref, tail_ref, wrecv, xs, hankel, invb, tf, lhs, own, exs, exr, us, ur, ds_, dr,
    fsend, frecv,
    l_sem, w_ss, w_rs, e_ss, e_rs, u_ss, u_rs, d_ss, d_rs, f_ss, f_rs,
):
    t = lax.axis_index("tm")
    s = lax.axis_index("sta")
    h = s // 16
    z = (s // 2) % 8
    c = s % 2
    sib = h * 16 + z * 2 + (1 - c)
    up = h * 16 + ((z + 1) % 8) * 2 + c
    down = h * 16 + ((z + 7) % 8) * 2 + c
    across = (1 - h) * 16 + z * 2 + c

    locals_ = [
        pltpu.make_async_copy(src, dst, l_sem.at[i])
        for i, (src, dst) in enumerate(
            ((wav_hbm, wav_ref), (tail_hbm, tail_ref), (mask_hbm, mask_ref), (tpl_hbm, tpl_ref))
        )
    ]
    for cp in locals_:
        cp.start()
    barrier = pltpu.get_barrier_semaphore()
    for step in range(1, UNITS):
        pl.semaphore_signal(barrier, inc=1, device_id=((t + step) % UNITS, s), device_id_type=MESH)
    for step in range(UNITS):
        pl.semaphore_signal(barrier, inc=1, device_id=((t + step) % UNITS, across), device_id_type=MESH)
    for other in (sib, up, down):
        pl.semaphore_signal(barrier, inc=1, device_id=(t, other), device_id_type=MESH)
    xs[...] = jnp.zeros((8, WIDE), jnp.float32)
    for cp in locals_:
        cp.wait()

    maskf = mask_ref[...].astype(jnp.float32)

    def templates(comp):
        values = tpl_ref[comp].astype(jnp.float32)
        mean = jnp.sum(values, axis=0, keepdims=True) / LAGS
        centred = values - mean
        energy = jnp.sum(centred * centred, axis=0, keepdims=True)
        normed = centred * lax.rsqrt(energy + 1e-05) * maskf
        padded = jnp.concatenate([normed, jnp.zeros((KPAD - LAGS, 256), jnp.float32)], axis=0)
        tf[comp] = padded.T
        for o in range(2):
            for d in range(8):
                zz = (z + d) % 8
                cc = c if o == 0 else 1 - c
                first = pl.multiple_of((h * 16 + zz * 2 + cc) * 8, 8)
                second = pl.multiple_of(((1 - h) * 16 + zz * 2 + cc) * 8, 8)
                both = jnp.concatenate([tf[comp, pl.ds(first, 8), :], tf[comp, pl.ds(second, 8), :]], axis=0)
                lhs[comp, 16 * (8 * o + d) : 16 * (8 * o + d) + 16, :] = both.astype(jnp.bfloat16)

    def place(value, start, width):
        v = value.astype(jnp.float32)
        xs[0:3, pl.ds(start, width)] = v
        xs[4:7, pl.ds(start, width)] = v * v

    templates(0)
    pl.semaphore_wait(barrier, 18)

    def remote(src, dst, ssem, rsem, dev):
        return pltpu.make_async_remote_copy(
            src_ref=src, dst_ref=dst, send_sem=ssem, recv_sem=rsem, device_id=dev, device_id_type=MESH
        )

    started = []

    def begin(cp):
        cp.start()
        started.append(cp)

    wcopies = [
        remote(wav_ref, wrecv.at[k], w_ss.at[k], w_rs.at[k], ((t + k) % UNITS, s)) for k in range(1, UNITS)
    ]
    for cp in wcopies:
        begin(cp)
    templates(1)
    templates(2)
    place(wav_ref[...], pl.multiple_of(t * CHUNK, 128), CHUNK)
    place(tail_ref[...], 8 * CHUNK, LAGS - 1)
    for k in range(1, UNITS):
        wcopies[k - 1].wait_recv()
        place(wrecv[k], pl.multiple_of(((t + UNITS - k) % UNITS) * CHUNK, 128), CHUNK)

    def window(at):
        a = xs[:, at : at + 1664]

        def ahead(v, n):
            return pltpu.roll(v, 1664 - n, axis=1)

        sums = {1: a}
        n = 1
        while n < 512:
            sums[2 * n] = sums[n] + ahead(sums[n], n)
            n *= 2
        total = sums[512] + ahead(sums[64], 512) + ahead(sums[16], 576) + ahead(sums[8], 592)
        total = total[:, :1024]
        squares = pltpu.roll(total, 4, axis=0)
        inverse = lax.rsqrt(squares - total * total / LAGS + 1e-05)
        for comp in range(3):
            invb[comp, :, at : at + 1024] = jnp.broadcast_to(inverse[comp : comp + 1], (8, 1024))

    def prepare(first, blocks):
        width = 128 * (blocks + 1)
        sub = lax.broadcasted_iota(jnp.int32, (8, width), 0)
        at = 128 * first
        for comp in range(3):
            v = jnp.broadcast_to(xs[comp : comp + 1, at : at + width], (8, width))
            for bit in (1, 2, 4):
                v = jnp.where((sub & bit) != 0, pltpu.roll(v, width - bit, axis=1), v)
            v = jnp.concatenate([v, pltpu.roll(v, width - 8, axis=1)], axis=0).astype(jnp.bfloat16)
            for m in range(8):
                both = v if m == 0 else pltpu.roll(v, width - 16 * m, axis=1)
                for q in range(blocks):
                    hankel[comp, at + 128 * q + 16 * m : at + 128 * q + 16 * m + 16, :] = both[
                        :, 128 * q : 128 * q + 128
                    ]

    origin = (s // 32) * 128

    def tile(i):
        at = pl.multiple_of(origin + 256 * i, 128)
        acc = None
        for comp in range(3):
            rhs = jnp.concatenate(
                [hankel[comp, pl.ds(pl.multiple_of(at + 128 * j, 128), KPAD), :] for j in range(2)], axis=1
            )
            prod = jnp.dot(lhs[comp], rhs, preferred_element_type=jnp.float32)
            prod = prod.reshape(32, 8, 256) * invb[comp, :, pl.ds(at, 256)][None]
            acc = prod if acc is None else acc + prod
        acc = acc.reshape(256, 256)
        for j in range(2):
            u, inside = divmod(2 * i + j, 7)
            own[u, :, 128 * inside : 128 * inside + 128] = acc[:128, 128 * j : 128 * j + 128]
            exs[u, :, 128 * inside : 128 * inside + 128] = acc[128:, 128 * j : 128 * j + 128].astype(jnp.bfloat16)
        if i % 7 in (3, 6):
            begin(exchange((2 * i + 1) // 7 - (1 if i % 7 == 3 else 0)))

    def exchange(u):
        return remote(exs.at[u], exr.at[u], e_ss.at[u], e_rs.at[u], (t, sib))

    def upward(u, k):
        return remote(us.at[u, k], ur.at[u, k], u_ss.at[u, k], u_rs.at[u, k], (t, up))

    def downward(u, k):
        return remote(ds_.at[u, k], dr.at[u, k], d_ss.at[u, k], d_rs.at[u, k], (t, down))

    def chunk(u, d):
        return own[u, 16 * d : 16 * d + 16, :] + exr[u, 16 * d : 16 * d + 16, :].astype(jnp.float32)

    def final(e, u, owner):
        return remote(
            fsend.at[e, u], frecv.at[e, t], f_ss.at[e, u], f_rs.at[e, t], (owner, s if e == 0 else across)
        )

    def stage(u, k):
        long_up = u % 2 == 0
        ways = (
            (upward, us, ur, 4 if long_up else 3, -1),
            (downward, ds_, dr, 3 if long_up else 4, 1),
        )
        if k == 1:
            exchange(u).wait_recv()
        if k <= 4:
            for way, send, recv, hops, sign in ways:
                if k <= hops:
                    left = hops - k + 1
                    v = chunk(u, left if sign < 0 else 8 - left)
                    if k > 1:
                        way(u, k - 2).wait_recv()
                        v = v + recv[u, k - 2].astype(jnp.float32)
                    send[u, k - 1] = v.astype(jnp.bfloat16)
                    begin(way(u, k - 1))
        else:
            v = chunk(u, 0)
            for way, send, recv, hops, sign in ways:
                way(u, hops - 1).wait_recv()
                v = v + recv[u, hops - 1].astype(jnp.float32)
            fsend[0, u] = v[:8]
            fsend[1, u] = v[8:]

            @pl.when(t != u)
            def _():
                final(0, u, u).start()

            @pl.when(t == u)
            def _():
                frecv[0, u] = v[:8]

            final(1, u, u).start()

    for k in range(7):
        window(1024 * k)
    prepare(0, BLOCKS)
    for what in order_of_work():
        if what[0] == "tile":
            tile(what[1])
        else:
            stage(what[1], what[2])

    for u in range(UNITS):
        def arrival(e, u=u):
            return remote(fsend.at[e, u], frecv.at[e, u], f_ss.at[e, u], f_rs.at[e, u], (u, s if e == 0 else across))

        @pl.when(t != u)
        def _():
            arrival(0).wait()

        arrival(1).wait()
        out_ref[u] = frecv[0, u] + frecv[1, u]
    for cp in started:
        cp.wait_send()


def per_device(templates, channel_mask, waveforms, waveform_tail):
    tpl = jnp.transpose(templates[0, :, 0], (1, 2, 0))
    mask = channel_mask.reshape(1, 256)
    bf, f32 = jnp.bfloat16, jnp.float32
    dma = pltpu.SemaphoreType.DMA
    anywhere = pl.BlockSpec(memory_space=pl.ANY)
    return pl.pallas_call(
        kernel,
        out_shape=jax.ShapeDtypeStruct((UNITS, 8, CHUNK), f32),
        in_specs=[anywhere] * 4,
        out_specs=pl.BlockSpec(memory_space=pltpu.VMEM),
        scratch_shapes=[
            pltpu.VMEM((3, LAGS, 256), bf),
            pltpu.VMEM((1, 256), jnp.int32),
            pltpu.VMEM((3, CHUNK), bf),
            pltpu.VMEM((3, LAGS - 1), bf),
            pltpu.VMEM((UNITS, 3, CHUNK), bf),
            pltpu.VMEM((8, WIDE), f32),
            pltpu.VMEM((3, 128 * BLOCKS, 128), bf),
            pltpu.VMEM((3, 8, UNITS * CHUNK), f32),
            pltpu.VMEM((3, 256, KPAD), f32),
            pltpu.VMEM((3, 256, KPAD), bf),
            pltpu.VMEM((UNITS, 128, CHUNK), f32),
            pltpu.VMEM((UNITS, 128, CHUNK), bf),
            pltpu.VMEM((UNITS, 128, CHUNK), bf),
            pltpu.VMEM((UNITS, 4, 16, CHUNK), bf),
            pltpu.VMEM((UNITS, 4, 16, CHUNK), bf),
            pltpu.VMEM((UNITS, 4, 16, CHUNK), bf),
            pltpu.VMEM((UNITS, 4, 16, CHUNK), bf),
            pltpu.VMEM((2, UNITS, 8, CHUNK), f32),
            pltpu.VMEM((2, UNITS, 8, CHUNK), f32),
            dma((4,)),
            dma((UNITS,)), dma((UNITS,)),
            dma((UNITS,)), dma((UNITS,)),
            dma((UNITS, 4)), dma((UNITS, 4)),
            dma((UNITS, 4)), dma((UNITS, 4)),
            dma((2, UNITS)), dma((2, UNITS)),
        ],
        compiler_params=pltpu.CompilerParams(
            collective_id=0, has_side_effects=True, vmem_limit_bytes=50 * 1024 * 1024
        ),
    )(tpl, mask, waveforms[0], waveform_tail[0])


def solution(mesh):
    placed = (
        P("tm", None, "sta", None, None),
        P("tm", None, "sta"),
        P("sta", None, "tm"),
        P("sta", None, None),
    )
    return jax.shard_map(
        per_device, mesh=mesh, in_specs=placed, out_specs=P(None, "sta", "tm"), check_vma=False
    )
```

```python
import jax
import jax.numpy as jnp
from jax import lax
from jax.experimental import pallas as pl
from jax.experimental.pallas import tpu as pltpu
from jax.sharding import PartitionSpec as P

MESH = pl.DeviceIdType.MESH
LAGS = 600
KPAD = 640
CHUNK = 896
UNITS = 8
TILES = 28
WIDE = 7936
BLOCKS = 60
TILE_US, EXCHANGE_US, HOP_US, QUEUE_US = 0.35, 1.5, 3.2, 0.0


def order_of_work():
    events = [(TILE_US * i, 0, ("tile", i)) for i in range(TILES)]
    for u in range(UNITS):
        done = TILE_US * (7 * (u // 2) + (4 if u % 2 == 0 else 7))
        for k in range(1, 6):
            when = done + EXCHANGE_US + HOP_US * (k - 1) + QUEUE_US * u * (k > 1)
            events.append((when, 1, ("stage", u, k)))
    return [e[2] for e in sorted(events, key=lambda e: (e[0], e[1], -e[2][-1]))]


def kernel(
    tpl_hbm, mask_hbm, wav_hbm, tail_hbm, out_ref,
    tpl_ref, mask_ref, wav_ref, tail_ref, wrecv, xs, hankel, invb, tf, lhs, own, exs, exr, us, ur, ds_, dr,
    fsend, frecv,
    l_sem, w_ss, w_rs, e_ss, e_rs, u_ss, u_rs, d_ss, d_rs, f_ss, f_rs,
):
    t = lax.axis_index("tm")
    s = lax.axis_index("sta")
    h = s // 16
    z = (s // 2) % 8
    c = s % 2
    sib = h * 16 + z * 2 + (1 - c)
    up = h * 16 + ((z + 1) % 8) * 2 + c
    down = h * 16 + ((z + 7) % 8) * 2 + c
    across = (1 - h) * 16 + z * 2 + c

    locals_ = [
        pltpu.make_async_copy(src, dst, l_sem.at[i])
        for i, (src, dst) in enumerate(
            ((wav_hbm, wav_ref), (tail_hbm, tail_ref), (mask_hbm, mask_ref), (tpl_hbm, tpl_ref))
        )
    ]
    for cp in locals_:
        cp.start()
    barrier = pltpu.get_barrier_semaphore()
    for step in range(1, UNITS):
        pl.semaphore_signal(barrier, inc=1, device_id=((t + step) % UNITS, s), device_id_type=MESH)
    for step in range(UNITS):
        pl.semaphore_signal(barrier, inc=1, device_id=((t + step) % UNITS, across), device_id_type=MESH)
    for other in (sib, up, down):
        pl.semaphore_signal(barrier, inc=1, device_id=(t, other), device_id_type=MESH)
    xs[...] = jnp.zeros((8, WIDE), jnp.float32)
    for cp in locals_:
        cp.wait()

    maskf = mask_ref[...].astype(jnp.float32)

    def templates(comp):
        values = tpl_ref[comp].astype(jnp.float32)
        mean = jnp.sum(values, axis=0, keepdims=True) / LAGS
        centred = values - mean
        energy = jnp.sum(centred * centred, axis=0, keepdims=True)
        normed = centred * lax.rsqrt(energy + 1e-05) * maskf
        padded = jnp.concatenate([normed, jnp.zeros((KPAD - LAGS, 256), jnp.float32)], axis=0)
        tf[comp] = padded.T
        for o in range(2):
            for d in range(8):
                zz = (z + d) % 8
                cc = c if o == 0 else 1 - c
                first = pl.multiple_of((h * 16 + zz * 2 + cc) * 8, 8)
                second = pl.multiple_of(((1 - h) * 16 + zz * 2 + cc) * 8, 8)
                both = jnp.concatenate([tf[comp, pl.ds(first, 8), :], tf[comp, pl.ds(second, 8), :]], axis=0)
                lhs[comp, 16 * (8 * o + d) : 16 * (8 * o + d) + 16, :] = both.astype(jnp.bfloat16)

    def place(value, start, width):
        v = value.astype(jnp.float32)
        xs[0:3, pl.ds(start, width)] = v
        xs[4:7, pl.ds(start, width)] = v * v

    templates(0)
    pl.semaphore_wait(barrier, 18)

    def remote(src, dst, ssem, rsem, dev):
        return pltpu.make_async_remote_copy(
            src_ref=src, dst_ref=dst, send_sem=ssem, recv_sem=rsem, device_id=dev, device_id_type=MESH
        )

    def begin(cp):
        cp.start()

    wcopies = [
        remote(wav_ref, wrecv.at[k], w_ss, w_rs.at[k], ((t + k) % UNITS, s)) for k in range(1, UNITS)
    ]
    for cp in wcopies:
        begin(cp)
    templates(1)
    templates(2)
    place(wav_ref[...], pl.multiple_of(t * CHUNK, 128), CHUNK)
    place(tail_ref[...], 8 * CHUNK, LAGS - 1)
    for k in range(1, UNITS):
        wcopies[k - 1].wait_recv()
        place(wrecv[k], pl.multiple_of(((t + UNITS - k) % UNITS) * CHUNK, 128), CHUNK)

    def window(at):
        a = xs[:, at : at + 1664]

        def ahead(v, n):
            return pltpu.roll(v, 1664 - n, axis=1)

        sums = {1: a}
        n = 1
        while n < 512:
            sums[2 * n] = sums[n] + ahead(sums[n], n)
            n *= 2
        total = sums[512] + ahead(sums[64], 512) + ahead(sums[16], 576) + ahead(sums[8], 592)
        total = total[:, :1024]
        squares = pltpu.roll(total, 4, axis=0)
        inverse = lax.rsqrt(squares - total * total / LAGS + 1e-05)
        for comp in range(3):
            invb[comp, :, at : at + 1024] = jnp.broadcast_to(inverse[comp : comp + 1], (8, 1024))

    def prepare(first, blocks):
        width = 128 * (blocks + 1)
        sub = lax.broadcasted_iota(jnp.int32, (8, width), 0)
        at = 128 * first
        for comp in range(3):
            v = jnp.broadcast_to(xs[comp : comp + 1, at : at + width], (8, width))
            for bit in (1, 2, 4):
                v = jnp.where((sub & bit) != 0, pltpu.roll(v, width - bit, axis=1), v)
            v = jnp.concatenate([v, pltpu.roll(v, width - 8, axis=1)], axis=0).astype(jnp.bfloat16)
            for m in range(8):
                both = v if m == 0 else pltpu.roll(v, width - 16 * m, axis=1)
                for q in range(blocks):
                    hankel[comp, at + 128 * q + 16 * m : at + 128 * q + 16 * m + 16, :] = both[
                        :, 128 * q : 128 * q + 128
                    ]

    origin = (s // 32) * 128

    def tile(i):
        at = pl.multiple_of(origin + 256 * i, 128)
        acc = None
        for comp in range(3):
            rhs = jnp.concatenate(
                [hankel[comp, pl.ds(pl.multiple_of(at + 128 * j, 128), KPAD), :] for j in range(2)], axis=1
            )
            prod = jnp.dot(lhs[comp], rhs, preferred_element_type=jnp.float32)
            prod = prod.reshape(32, 8, 256) * invb[comp, :, pl.ds(at, 256)][None]
            acc = prod if acc is None else acc + prod
        acc = acc.reshape(256, 256)
        for j in range(2):
            u, inside = divmod(2 * i + j, 7)
            own[u, :, 128 * inside : 128 * inside + 128] = acc[:128, 128 * j : 128 * j + 128]
            exs[u, :, 128 * inside : 128 * inside + 128] = acc[128:, 128 * j : 128 * j + 128]
        if i % 7 in (3, 6):
            begin(exchange((2 * i + 1) // 7 - (1 if i % 7 == 3 else 0)))

    def exchange(u):
        return remote(exs.at[u], exr.at[u], e_ss, e_rs.at[u], (t, sib))

    def up_slot(u, k):
        return 7 * (u // 2) + 4 * (u % 2) + k

    def down_slot(u, k):
        return 7 * (u // 2) + 3 * (u % 2) + k

    def upward(u, k):
        i = up_slot(u, k)
        return remote(us.at[i], ur.at[i], u_ss, u_rs.at[i], (t, up))

    def downward(u, k):
        i = down_slot(u, k)
        return remote(ds_.at[i], dr.at[i], d_ss, d_rs.at[i], (t, down))

    def chunk(u, d):
        return own[u, 16 * d : 16 * d + 16, :] + exr[u, 16 * d : 16 * d + 16, :]

    def final(e, u, owner):
        return remote(
            fsend.at[e, u], frecv.at[e, t], f_ss.at[e], f_rs.at[e, t], (owner, s if e == 0 else across)
        )

    def stage(u, k):
        long_up = u % 2 == 0
        ways = (
            (upward, up_slot, us, ur, 4 if long_up else 3, -1),
            (downward, down_slot, ds_, dr, 3 if long_up else 4, 1),
        )
        if k == 1:
            exchange(u).wait_recv()
        if k <= 4:
            for way, slot, send, recv, hops, sign in ways:
                if k <= hops:
                    left = hops - k + 1
                    v = chunk(u, left if sign < 0 else 8 - left)
                    if k > 1:
                        way(u, k - 2).wait_recv()
                        v = v + recv[slot(u, k - 2)].astype(jnp.float32)
                    send[slot(u, k - 1)] = v.astype(jnp.bfloat16)
                    begin(way(u, k - 1))
        else:
            v = chunk(u, 0)
            for way, slot, send, recv, hops, sign in ways:
                way(u, hops - 1).wait_recv()
                v = v + recv[slot(u, hops - 1)].astype(jnp.float32)
            fsend[0, u] = v[:8].astype(jnp.bfloat16)
            fsend[1, u] = v[8:].astype(jnp.bfloat16)

            @pl.when(t != u)
            def _():
                final(0, u, u).start()

            @pl.when(t == u)
            def _():
                frecv[0, u] = v[:8].astype(jnp.bfloat16)

            final(1, u, u).start()

    for k in range(7):
        window(1024 * k)
    prepare(0, BLOCKS)
    for what in order_of_work():
        if what[0] == "tile":
            tile(what[1])
            if what[1] == 3:
                pass
        else:
            stage(what[1], what[2])

    for u in range(UNITS):
        def arrival(e, u=u):
            return remote(fsend.at[e, u], frecv.at[e, u], f_ss.at[e], f_rs.at[e, u], (u, s if e == 0 else across))

        @pl.when(t != u)
        def _():
            arrival(0).wait_recv()

        arrival(1).wait_recv()
        out_ref[u] = frecv[0, u].astype(jnp.float32) + frecv[1, u].astype(jnp.float32)
    for sent, sem in (
        (wrecv.at[pl.ds(1, UNITS - 1)], w_ss),
        (exs, e_ss),
        (us, u_ss),
        (ds_, d_ss),
        (fsend.at[0, pl.ds(1, UNITS - 1)], f_ss.at[0]),
        (fsend.at[1], f_ss.at[1]),
    ):
        remote(sent, sent, sem, w_rs.at[0], (t, sib)).wait_send()


def per_device(templates, channel_mask, waveforms, waveform_tail):
    tpl = jnp.transpose(templates[0, :, 0], (1, 2, 0))
    mask = channel_mask.reshape(1, 256)
    bf, f32 = jnp.bfloat16, jnp.float32
    dma = pltpu.SemaphoreType.DMA
    anywhere = pl.BlockSpec(memory_space=pl.ANY)
    return pl.pallas_call(
        kernel,
        out_shape=jax.ShapeDtypeStruct((UNITS, 8, CHUNK), f32),
        in_specs=[anywhere] * 4,
        out_specs=pl.BlockSpec(memory_space=pltpu.VMEM),
        scratch_shapes=[
            pltpu.VMEM((3, LAGS, 256), bf),
            pltpu.VMEM((1, 256), jnp.int32),
            pltpu.VMEM((3, CHUNK), bf),
            pltpu.VMEM((3, LAGS - 1), bf),
            pltpu.VMEM((UNITS, 3, CHUNK), bf),
            pltpu.VMEM((8, WIDE), f32),
            pltpu.VMEM((3, 128 * BLOCKS, 128), bf),
            pltpu.VMEM((3, 8, UNITS * CHUNK), f32),
            pltpu.VMEM((3, 256, KPAD), f32),
            pltpu.VMEM((3, 256, KPAD), bf),
            pltpu.VMEM((UNITS, 128, CHUNK), f32),
            pltpu.VMEM((UNITS, 128, CHUNK), f32),
            pltpu.VMEM((UNITS, 128, CHUNK), f32),
            pltpu.VMEM((28, 16, CHUNK), bf),
            pltpu.VMEM((28, 16, CHUNK), bf),
            pltpu.VMEM((28, 16, CHUNK), bf),
            pltpu.VMEM((28, 16, CHUNK), bf),
            pltpu.VMEM((2, UNITS, 8, CHUNK), bf),
            pltpu.VMEM((2, UNITS, 8, CHUNK), bf),
            dma((4,)),
            dma, dma((UNITS,)),
            dma, dma((UNITS,)),
            dma, dma((28,)),
            dma, dma((28,)),
            dma((2,)), dma((2, UNITS)),
        ],
        compiler_params=pltpu.CompilerParams(
            collective_id=0, has_side_effects=True, vmem_limit_bytes=50 * 1024 * 1024
        ),
    )(tpl, mask, waveforms[0], waveform_tail[0])


def solution(mesh):
    placed = (
        P("tm", None, "sta", None, None),
        P("tm", None, "sta"),
        P("sta", None, "tm"),
        P("sta", None, None),
    )
    return jax.shard_map(
        per_device, mesh=mesh, in_specs=placed, out_specs=P(None, "sta", "tm"), check_vma=False
    )
```

```python
import jax
import jax.numpy as jnp
from jax import lax
from jax.experimental import pallas as pl
from jax.experimental.pallas import tpu as pltpu
from jax.sharding import PartitionSpec as P

MESH = pl.DeviceIdType.MESH
LAGS = 600
KPAD = 640
CHUNK = 896
UNITS = 8
TILES = 28
WIDE = 7936
BLOCKS = 60
TILE_US, EXCHANGE_US, HOP_US, QUEUE_US = 0.35, 1.5, 3.2, 0.0


def order_of_work():
    events = [(TILE_US * i, 0, ("tile", i)) for i in range(TILES)]
    for u in range(UNITS):
        done = TILE_US * (7 * (u // 2) + (4 if u % 2 == 0 else 7))
        for k in range(1, 6):
            when = done + EXCHANGE_US + HOP_US * (k - 1) + QUEUE_US * u * (k > 1)
            events.append((when, 1, ("stage", u, k)))
    return [e[2] for e in sorted(events, key=lambda e: (e[0], e[1], -e[2][-1]))]


def kernel(
    tpl_hbm, mask_hbm, wav_hbm, tail_hbm, out_ref,
    tpl_ref, mask_ref, wav_ref, tail_ref, wrecv, xs, hankel, invb, tf, lhs, own, exs, exr, us, ur, ds_, dr,
    fsend, frecv,
    l_sem, w_ss, w_rs, e_ss, e_rs, u_ss, u_rs, d_ss, d_rs, f_ss, f_rs,
):
    t = lax.axis_index("tm")
    s = lax.axis_index("sta")
    h = s // 16
    z = (s // 2) % 8
    c = s % 2
    sib = h * 16 + z * 2 + (1 - c)
    up = h * 16 + ((z + 1) % 8) * 2 + c
    down = h * 16 + ((z + 7) % 8) * 2 + c
    across = (1 - h) * 16 + z * 2 + c

    locals_ = [
        pltpu.make_async_copy(src, dst, l_sem.at[i])
        for i, (src, dst) in enumerate(
            ((wav_hbm, wav_ref), (tail_hbm, tail_ref), (mask_hbm, mask_ref), (tpl_hbm, tpl_ref))
        )
    ]
    for cp in locals_:
        cp.start()
    barrier = pltpu.get_barrier_semaphore()
    for step in range(1, UNITS):
        pl.semaphore_signal(barrier, inc=1, device_id=((t + step) % UNITS, s), device_id_type=MESH)
    for step in range(UNITS):
        pl.semaphore_signal(barrier, inc=1, device_id=((t + step) % UNITS, across), device_id_type=MESH)
    for other in (sib, up, down):
        pl.semaphore_signal(barrier, inc=1, device_id=(t, other), device_id_type=MESH)
    xs[...] = jnp.zeros((8, WIDE), jnp.float32)
    for cp in locals_:
        cp.wait()

    maskf = mask_ref[...].astype(jnp.float32)

    def templates(comp):
        values = tpl_ref[comp].astype(jnp.float32)
        mean = jnp.sum(values, axis=0, keepdims=True) / LAGS
        centred = values - mean
        energy = jnp.sum(centred * centred, axis=0, keepdims=True)
        normed = centred * lax.rsqrt(energy + 1e-05) * maskf
        padded = jnp.concatenate([normed, jnp.zeros((KPAD - LAGS, 256), jnp.float32)], axis=0)
        tf[comp] = padded.T
        for o in range(2):
            for d in range(8):
                zz = (z + d) % 8
                cc = c if o == 0 else 1 - c
                first = pl.multiple_of((h * 16 + zz * 2 + cc) * 8, 8)
                second = pl.multiple_of(((1 - h) * 16 + zz * 2 + cc) * 8, 8)
                both = jnp.concatenate([tf[comp, pl.ds(first, 8), :], tf[comp, pl.ds(second, 8), :]], axis=0)
                lhs[comp, 16 * (8 * o + d) : 16 * (8 * o + d) + 16, :] = both.astype(jnp.bfloat16)

    def place(value, start, width):
        v = value.astype(jnp.float32)
        xs[0:3, pl.ds(start, width)] = v
        xs[4:7, pl.ds(start, width)] = v * v

    templates(0)
    pl.semaphore_wait(barrier, 18)

    def remote(src, dst, ssem, rsem, dev):
        return pltpu.make_async_remote_copy(
            src_ref=src, dst_ref=dst, send_sem=ssem, recv_sem=rsem, device_id=dev, device_id_type=MESH
        )

    def begin(cp):
        cp.start()

    wcopies = [
        remote(wav_ref, wrecv.at[k], w_ss, w_rs.at[k], ((t + k) % UNITS, s)) for k in range(1, UNITS)
    ]
    for cp in wcopies:
        begin(cp)
    templates(1)
    templates(2)
    place(wav_ref[...], pl.multiple_of(t * CHUNK, 128), CHUNK)
    place(tail_ref[...], 8 * CHUNK, LAGS - 1)
    for k in range(1, UNITS):
        wcopies[k - 1].wait_recv()
        place(wrecv[k], pl.multiple_of(((t + UNITS - k) % UNITS) * CHUNK, 128), CHUNK)

    def window(at):
        a = xs[:, at : at + 1664]

        def ahead(v, n):
            return pltpu.roll(v, 1664 - n, axis=1)

        sums = {1: a}
        n = 1
        while n < 512:
            sums[2 * n] = sums[n] + ahead(sums[n], n)
            n *= 2
        total = sums[512] + ahead(sums[64], 512) + ahead(sums[16], 576) + ahead(sums[8], 592)
        total = total[:, :1024]
        squares = pltpu.roll(total, 4, axis=0)
        inverse = lax.rsqrt(squares - total * total / LAGS + 1e-05)
        for comp in range(3):
            invb[comp, :, at : at + 1024] = jnp.broadcast_to(inverse[comp : comp + 1], (8, 1024))

    def prepare(first, blocks):
        width = 128 * (blocks + 1)
        sub = lax.broadcasted_iota(jnp.int32, (8, width), 0)
        at = 128 * first
        for comp in range(3):
            v = jnp.broadcast_to(xs[comp : comp + 1, at : at + width], (8, width))
            for bit in (1, 2, 4):
                v = jnp.where((sub & bit) != 0, pltpu.roll(v, width - bit, axis=1), v)
            v = jnp.concatenate([v, pltpu.roll(v, width - 8, axis=1)], axis=0).astype(jnp.bfloat16)
            for m in range(8):
                both = v if m == 0 else pltpu.roll(v, width - 16 * m, axis=1)
                for q in range(blocks):
                    hankel[comp, at + 128 * q + 16 * m : at + 128 * q + 16 * m + 16, :] = both[
                        :, 128 * q : 128 * q + 128
                    ]

    origin = (s // 32) * 128

    def tile(i):
        at = pl.multiple_of(origin + 256 * i, 128)
        acc = None
        for comp in range(3):
            rhs = jnp.concatenate(
                [hankel[comp, pl.ds(pl.multiple_of(at + 128 * j, 128), KPAD), :] for j in range(2)], axis=1
            )
            prod = jnp.dot(lhs[comp], rhs, preferred_element_type=jnp.float32)
            prod = prod.reshape(32, 8, 256) * invb[comp, :, pl.ds(at, 256)][None]
            acc = prod if acc is None else acc + prod
        acc = acc.reshape(256, 256)
        for j in range(2):
            u, inside = divmod(2 * i + j, 7)
            own[u, :, 128 * inside : 128 * inside + 128] = acc[:128, 128 * j : 128 * j + 128]
            exs[u, :, 128 * inside : 128 * inside + 128] = acc[128:, 128 * j : 128 * j + 128]
        if i % 7 in (3, 6):
            begin(exchange((2 * i + 1) // 7 - (1 if i % 7 == 3 else 0)))

    def exchange(u):
        return remote(exs.at[u], exr.at[u], e_ss, e_rs.at[u], (t, sib))

    def up_slot(u, k):
        return 7 * (u // 2) + 4 * (u % 2) + k

    def down_slot(u, k):
        return 7 * (u // 2) + 3 * (u % 2) + k

    def upward(u, k):
        i = up_slot(u, k)
        return remote(us.at[i], ur.at[i], u_ss, u_rs.at[i], (t, up))

    def downward(u, k):
        i = down_slot(u, k)
        return remote(ds_.at[i], dr.at[i], d_ss, d_rs.at[i], (t, down))

    def chunk(u, d):
        return own[u, 16 * d : 16 * d + 16, :] + exr[u, 16 * d : 16 * d + 16, :]

    def final(e, u, owner):
        return remote(
            fsend.at[e, u], frecv.at[e, t], f_ss.at[e], f_rs.at[e, t], (owner, s if e == 0 else across)
        )

    def stage(u, k):
        long_up = u % 2 == 0
        ways = (
            (upward, up_slot, us, ur, 4 if long_up else 3, -1),
            (downward, down_slot, ds_, dr, 3 if long_up else 4, 1),
        )
        if k == 1:
            exchange(u).wait_recv()
        if k <= 4:
            for way, slot, send, recv, hops, sign in ways:
                if k <= hops:
                    left = hops - k + 1
                    v = chunk(u, left if sign < 0 else 8 - left)
                    if k > 1:
                        way(u, k - 2).wait_recv()
                        v = v + recv[slot(u, k - 2)].astype(jnp.float32)
                    send[slot(u, k - 1)] = v.astype(jnp.bfloat16)
                    begin(way(u, k - 1))
        else:
            v = chunk(u, 0)
            for way, slot, send, recv, hops, sign in ways:
                way(u, hops - 1).wait_recv()
                v = v + recv[slot(u, hops - 1)].astype(jnp.float32)
            fsend[0, u] = v[:8].astype(jnp.bfloat16)
            fsend[1, u] = v[8:].astype(jnp.bfloat16)

            @pl.when(t != u)
            def _():
                final(0, u, u).start()

            @pl.when(t == u)
            def _():
                frecv[0, u] = v[:8].astype(jnp.bfloat16)

            final(1, u, u).start()

    for k in range(7):
        window(1024 * k)
    prepare(0, BLOCKS)
    for what in order_of_work():
        if what[0] == "tile":
            tile(what[1])
            if what[1] == 3:
                pass
        else:
            stage(what[1], what[2])

    for u in range(UNITS):
        def arrival(e, u=u):
            return remote(fsend.at[e, u], frecv.at[e, u], f_ss.at[e], f_rs.at[e, u], (u, s if e == 0 else across))

        @pl.when(t != u)
        def _():
            arrival(0).wait_recv()

        arrival(1).wait_recv()
        out_ref[u] = frecv[0, u].astype(jnp.float32) + frecv[1, u].astype(jnp.float32)
    for sent, sem in (
        (wrecv.at[pl.ds(1, UNITS - 1)], w_ss),
        (exs, e_ss),
        (us, u_ss),
        (ds_, d_ss),
        (fsend.at[0, pl.ds(1, UNITS - 1)], f_ss.at[0]),
        (fsend.at[1], f_ss.at[1]),
    ):
        remote(sent, sent, sem, w_rs.at[0], (t, sib)).wait_send()


def per_device(templates, channel_mask, waveforms, waveform_tail):
    tpl = jnp.transpose(templates[0, :, 0], (1, 2, 0))
    mask = channel_mask.reshape(1, 256)
    bf, f32 = jnp.bfloat16, jnp.float32
    dma = pltpu.SemaphoreType.DMA
    anywhere = pl.BlockSpec(memory_space=pl.ANY)
    return pl.pallas_call(
        kernel,
        out_shape=jax.ShapeDtypeStruct((UNITS, 8, CHUNK), f32),
        in_specs=[anywhere] * 4,
        out_specs=pl.BlockSpec(memory_space=pltpu.VMEM),
        scratch_shapes=[
            pltpu.VMEM((3, LAGS, 256), bf),
            pltpu.VMEM((1, 256), jnp.int32),
            pltpu.VMEM((3, CHUNK), bf),
            pltpu.VMEM((3, LAGS - 1), bf),
            pltpu.VMEM((UNITS, 3, CHUNK), bf),
            pltpu.VMEM((8, WIDE), f32),
            pltpu.VMEM((3, 128 * BLOCKS, 128), bf),
            pltpu.VMEM((3, 8, UNITS * CHUNK), f32),
            pltpu.VMEM((3, 256, KPAD), f32),
            pltpu.VMEM((3, 256, KPAD), bf),
            pltpu.VMEM((UNITS, 128, CHUNK), f32),
            pltpu.VMEM((UNITS, 128, CHUNK), f32),
            pltpu.VMEM((UNITS, 128, CHUNK), f32),
            pltpu.VMEM((28, 16, CHUNK), bf),
            pltpu.VMEM((28, 16, CHUNK), bf),
            pltpu.VMEM((28, 16, CHUNK), bf),
            pltpu.VMEM((28, 16, CHUNK), bf),
            pltpu.VMEM((2, UNITS, 8, CHUNK), bf),
            pltpu.VMEM((2, UNITS, 8, CHUNK), bf),
            dma((4,)),
            dma, dma((UNITS,)),
            dma, dma((UNITS,)),
            dma, dma((28,)),
            dma, dma((28,)),
            dma((2,)), dma((2, UNITS)),
        ],
        compiler_params=pltpu.CompilerParams(
            collective_id=0, has_side_effects=True
        ),
    )(tpl, mask, waveforms[0], waveform_tail[0])


def solution(mesh):
    placed = (
        P("tm", None, "sta", None, None),
        P("tm", None, "sta"),
        P("sta", None, "tm"),
        P("sta", None, None),
    )
    return jax.shard_map(
        per_device, mesh=mesh, in_specs=placed, out_specs=P(None, "sta", "tm"), check_vma=False
    )
```

```python
import jax
import jax.numpy as jnp
from jax import lax
from jax.experimental import pallas as pl
from jax.experimental.pallas import tpu as pltpu
from jax.sharding import PartitionSpec as P

MESH = pl.DeviceIdType.MESH
LAGS = 600
KPAD = 640
CHUNK = 896
UNITS = 8
TILES = 28
WIDE = 7936
BLOCKS = 60
TILE_US, EXCHANGE_US, HOP_US, QUEUE_US = 0.35, 1.5, 3.2, 0.0


def order_of_work():
    events = [(TILE_US * i, 0, ("tile", i)) for i in range(TILES)]
    for u in range(UNITS):
        done = TILE_US * (7 * (u // 2) + (4 if u % 2 == 0 else 7))
        for k in range(1, 6):
            when = done + EXCHANGE_US + HOP_US * (k - 1) + QUEUE_US * u * (k > 1)
            events.append((when, 1, ("stage", u, k)))
    return [e[2] for e in sorted(events, key=lambda e: (e[0], e[1], -e[2][-1]))]


def kernel(
    tpl_hbm, mask_hbm, wav_hbm, tail_hbm, out_ref,
    tpl_ref, mask_ref, wav_ref, tail_ref, wrecv, xs, hankel, invb, tf, lhs, own, exs, exr, us, ur, ds_, dr,
    fsend, frecv,
    l_sem, w_ss, w_rs, e_ss, e_rs, u_ss, u_rs, d_ss, d_rs, f_ss, f_rs,
):
    t = lax.axis_index("tm")
    s = lax.axis_index("sta")
    h = s // 16
    z = (s // 2) % 8
    c = s % 2
    sib = h * 16 + z * 2 + (1 - c)
    up = h * 16 + ((z + 1) % 8) * 2 + c
    down = h * 16 + ((z + 7) % 8) * 2 + c
    across = (1 - h) * 16 + z * 2 + c

    locals_ = [
        pltpu.make_async_copy(src, dst, l_sem.at[i])
        for i, (src, dst) in enumerate(
            ((wav_hbm, wav_ref), (tail_hbm, tail_ref), (mask_hbm, mask_ref), (tpl_hbm, tpl_ref))
        )
    ]
    for cp in locals_:
        cp.start()
    barrier = pltpu.get_barrier_semaphore()
    for step in range(1, UNITS):
        pl.semaphore_signal(barrier, inc=1, device_id=((t + step) % UNITS, s), device_id_type=MESH)
    for step in range(UNITS):
        pl.semaphore_signal(barrier, inc=1, device_id=((t + step) % UNITS, across), device_id_type=MESH)
    for other in (sib, up, down):
        pl.semaphore_signal(barrier, inc=1, device_id=(t, other), device_id_type=MESH)
    xs[...] = jnp.zeros((8, WIDE), jnp.float32)

    def templates(comp):
        values = tpl_ref[comp].astype(jnp.float32)
        mean = jnp.sum(values, axis=0, keepdims=True) / LAGS
        centred = values - mean
        energy = jnp.sum(centred * centred, axis=0, keepdims=True)
        normed = centred * lax.rsqrt(energy + 1e-05) * mask_ref[...].astype(jnp.float32)
        padded = jnp.concatenate([normed, jnp.zeros((KPAD - LAGS, 256), jnp.float32)], axis=0)
        tf[comp] = padded.T
        for o in range(2):
            for d in range(8):
                zz = (z + d) % 8
                cc = c if o == 0 else 1 - c
                first = pl.multiple_of((h * 16 + zz * 2 + cc) * 8, 8)
                second = pl.multiple_of(((1 - h) * 16 + zz * 2 + cc) * 8, 8)
                both = jnp.concatenate([tf[comp, pl.ds(first, 8), :], tf[comp, pl.ds(second, 8), :]], axis=0)
                lhs[comp, 16 * (8 * o + d) : 16 * (8 * o + d) + 16, :] = both.astype(jnp.bfloat16)

    def place(value, start, width):
        v = value.astype(jnp.float32)
        xs[0:3, pl.ds(start, width)] = v
        xs[4:7, pl.ds(start, width)] = v * v

    locals_[0].wait()
    pl.semaphore_wait(barrier, 18)

    def remote(src, dst, ssem, rsem, dev):
        return pltpu.make_async_remote_copy(
            src_ref=src, dst_ref=dst, send_sem=ssem, recv_sem=rsem, device_id=dev, device_id_type=MESH
        )

    def begin(cp):
        cp.start()

    wcopies = [
        remote(wav_ref, wrecv.at[k], w_ss, w_rs.at[k], ((t + k) % UNITS, s)) for k in range(1, UNITS)
    ]
    for cp in wcopies:
        begin(cp)
    for cp in locals_[1:]:
        cp.wait()
    for comp in range(3):
        templates(comp)
    place(wav_ref[...], pl.multiple_of(t * CHUNK, 128), CHUNK)
    place(tail_ref[...], 8 * CHUNK, LAGS - 1)
    for k in range(1, UNITS):
        wcopies[k - 1].wait_recv()
        place(wrecv[k], pl.multiple_of(((t + UNITS - k) % UNITS) * CHUNK, 128), CHUNK)

    def window(at):
        a = xs[:, at : at + 1664]

        def ahead(v, n):
            return pltpu.roll(v, 1664 - n, axis=1)

        sums = {1: a}
        n = 1
        while n < 512:
            sums[2 * n] = sums[n] + ahead(sums[n], n)
            n *= 2
        total = sums[512] + ahead(sums[64], 512) + ahead(sums[16], 576) + ahead(sums[8], 592)
        total = total[:, :1024]
        squares = pltpu.roll(total, 4, axis=0)
        inverse = lax.rsqrt(squares - total * total / LAGS + 1e-05)
        for comp in range(3):
            invb[comp, :, at : at + 1024] = jnp.broadcast_to(inverse[comp : comp + 1], (8, 1024))

    def prepare(first, blocks):
        width = 128 * (blocks + 1)
        sub = lax.broadcasted_iota(jnp.int32, (8, width), 0)
        at = 128 * first
        for comp in range(3):
            v = jnp.broadcast_to(xs[comp : comp + 1, at : at + width], (8, width))
            for bit in (1, 2, 4):
                v = jnp.where((sub & bit) != 0, pltpu.roll(v, width - bit, axis=1), v)
            v = jnp.concatenate([v, pltpu.roll(v, width - 8, axis=1)], axis=0).astype(jnp.bfloat16)
            for m in range(8):
                both = v if m == 0 else pltpu.roll(v, width - 16 * m, axis=1)
                for q in range(blocks):
                    hankel[comp, at + 128 * q + 16 * m : at + 128 * q + 16 * m + 16, :] = both[
                        :, 128 * q : 128 * q + 128
                    ]

    origin = (s // 32) * 128

    def tile(i):
        at = pl.multiple_of(origin + 256 * i, 128)
        acc = None
        for comp in range(3):
            rhs = jnp.concatenate(
                [hankel[comp, pl.ds(pl.multiple_of(at + 128 * j, 128), KPAD), :] for j in range(2)], axis=1
            )
            prod = jnp.dot(lhs[comp], rhs, preferred_element_type=jnp.float32)
            prod = prod.reshape(32, 8, 256) * invb[comp, :, pl.ds(at, 256)][None]
            acc = prod if acc is None else acc + prod
        acc = acc.reshape(256, 256)
        for j in range(2):
            u, inside = divmod(2 * i + j, 7)
            own[u, :, 128 * inside : 128 * inside + 128] = acc[:128, 128 * j : 128 * j + 128]
            exs[u, :, 128 * inside : 128 * inside + 128] = acc[128:, 128 * j : 128 * j + 128]
        if i % 7 in (3, 6):
            begin(exchange((2 * i + 1) // 7 - (1 if i % 7 == 3 else 0)))

    def exchange(u):
        return remote(exs.at[u], exr.at[u], e_ss, e_rs.at[u], (t, sib))

    def up_slot(u, k):
        return 7 * (u // 2) + 4 * (u % 2) + k

    def down_slot(u, k):
        return 7 * (u // 2) + 3 * (u % 2) + k

    def upward(u, k):
        i = up_slot(u, k)
        return remote(us.at[i], ur.at[i], u_ss, u_rs.at[i], (t, up))

    def downward(u, k):
        i = down_slot(u, k)
        return remote(ds_.at[i], dr.at[i], d_ss, d_rs.at[i], (t, down))

    def chunk(u, d):
        return own[u, 16 * d : 16 * d + 16, :] + exr[u, 16 * d : 16 * d + 16, :]

    def final(e, u, owner):
        return remote(
            fsend.at[e, u], frecv.at[e, t], f_ss.at[e], f_rs.at[e, t], (owner, s if e == 0 else across)
        )

    def stage(u, k):
        long_up = u % 2 == 0
        ways = (
            (upward, up_slot, us, ur, 4 if long_up else 3, -1),
            (downward, down_slot, ds_, dr, 3 if long_up else 4, 1),
        )
        if k == 1:
            exchange(u).wait_recv()
        if k <= 4:
            for way, slot, send, recv, hops, sign in ways:
                if k <= hops:
                    left = hops - k + 1
                    v = chunk(u, left if sign < 0 else 8 - left)
                    if k > 1:
                        way(u, k - 2).wait_recv()
                        v = v + recv[slot(u, k - 2)].astype(jnp.float32)
                    send[slot(u, k - 1)] = v.astype(jnp.bfloat16)
                    begin(way(u, k - 1))
        else:
            v = chunk(u, 0)
            for way, slot, send, recv, hops, sign in ways:
                way(u, hops - 1).wait_recv()
                v = v + recv[slot(u, hops - 1)].astype(jnp.float32)
            fsend[0, u] = v[:8].astype(jnp.bfloat16)
            fsend[1, u] = v[8:].astype(jnp.bfloat16)

            @pl.when(t != u)
            def _():
                final(0, u, u).start()

            @pl.when(t == u)
            def _():
                frecv[0, u] = v[:8].astype(jnp.bfloat16)

            final(1, u, u).start()

    for k in range(7):
        window(1024 * k)
    prepare(0, BLOCKS)
    for what in order_of_work():
        if what[0] == "tile":
            tile(what[1])
            if what[1] == 3:
                pass
        else:
            stage(what[1], what[2])

    for u in range(UNITS):
        def arrival(e, u=u):
            return remote(fsend.at[e, u], frecv.at[e, u], f_ss.at[e], f_rs.at[e, u], (u, s if e == 0 else across))

        @pl.when(t != u)
        def _():
            arrival(0).wait_recv()

        arrival(1).wait_recv()
        out_ref[u] = frecv[0, u].astype(jnp.float32) + frecv[1, u].astype(jnp.float32)
    for sent, sem in (
        (wrecv.at[pl.ds(1, UNITS - 1)], w_ss),
        (exs, e_ss),
        (us, u_ss),
        (ds_, d_ss),
        (fsend.at[0, pl.ds(1, UNITS - 1)], f_ss.at[0]),
        (fsend.at[1], f_ss.at[1]),
    ):
        remote(sent, sent, sem, w_rs.at[0], (t, sib)).wait_send()


def per_device(templates, channel_mask, waveforms, waveform_tail):
    tpl = jnp.transpose(templates[0, :, 0], (1, 2, 0))
    mask = channel_mask.reshape(1, 256)
    bf, f32 = jnp.bfloat16, jnp.float32
    dma = pltpu.SemaphoreType.DMA
    anywhere = pl.BlockSpec(memory_space=pl.ANY)
    return pl.pallas_call(
        kernel,
        out_shape=jax.ShapeDtypeStruct((UNITS, 8, CHUNK), f32),
        in_specs=[anywhere] * 4,
        out_specs=pl.BlockSpec(memory_space=pltpu.VMEM),
        scratch_shapes=[
            pltpu.VMEM((3, LAGS, 256), bf),
            pltpu.VMEM((1, 256), jnp.int32),
            pltpu.VMEM((3, CHUNK), bf),
            pltpu.VMEM((3, LAGS - 1), bf),
            pltpu.VMEM((UNITS, 3, CHUNK), bf),
            pltpu.VMEM((8, WIDE), f32),
            pltpu.VMEM((3, 128 * BLOCKS, 128), bf),
            pltpu.VMEM((3, 8, UNITS * CHUNK), f32),
            pltpu.VMEM((3, 256, KPAD), f32),
            pltpu.VMEM((3, 256, KPAD), bf),
            pltpu.VMEM((UNITS, 128, CHUNK), f32),
            pltpu.VMEM((UNITS, 128, CHUNK), f32),
            pltpu.VMEM((UNITS, 128, CHUNK), f32),
            pltpu.VMEM((28, 16, CHUNK), bf),
            pltpu.VMEM((28, 16, CHUNK), bf),
            pltpu.VMEM((28, 16, CHUNK), bf),
            pltpu.VMEM((28, 16, CHUNK), bf),
            pltpu.VMEM((2, UNITS, 8, CHUNK), bf),
            pltpu.VMEM((2, UNITS, 8, CHUNK), bf),
            dma((4,)),
            dma, dma((UNITS,)),
            dma, dma((UNITS,)),
            dma, dma((28,)),
            dma, dma((28,)),
            dma((2,)), dma((2, UNITS)),
        ],
        compiler_params=pltpu.CompilerParams(
            collective_id=0, has_side_effects=True
        ),
    )(tpl, mask, waveforms[0], waveform_tail[0])


def solution(mesh):
    placed = (
        P("tm", None, "sta", None, None),
        P("tm", None, "sta"),
        P("sta", None, "tm"),
        P("sta", None, None),
    )
    return jax.shard_map(
        per_device, mesh=mesh, in_specs=placed, out_specs=P(None, "sta", "tm"), check_vma=False
    )
```
